32 devices in a mesh: com: 4 (over x, core), arc: 8 (over z, y).
Axes of the slice: x: 2, y: 2, z: 4, core: 2. Of those that a mesh axis runs over, the one named last changes fastest.
Arguments:
- flows: float32 [8192, 4096], P('arc', 'com'), may hold values from -6 to 6
- duals: float32 [8192, 4096], P('arc', 'com'), may hold values from -6 to 6
- potentials: float32 [4096, 4096], P('arc', 'com'), may hold values from -6 to 6
- demand: float32 [4096, 4096], P('arc', 'com'), may hold values from -6 to 6
- arc_cost: float32 [8192], P('arc'), may hold values from 0.2 to 1
- cap_ratio: float32 [8192], P('arc'), may hold values from 0.6 to 2.6
- patterns: float32 [16, 128, 128], replicated, may hold values from -0.1875 to 0.1875
- nodes_of: int32 [64, 8], P('arc'), may hold values from 0 to 31, as said below
- pattern_of: int32 [64, 8], P('arc'), may hold values from 0 to 15
- scen_index: int32 [4096], replicated, may hold values from 0 to 7
- level_weights: float32 [8], replicated, may hold values from 0.5 to 2
Outputs:
- flows_out: float32 [8192, 4096], P('arc', 'com')
- duals_out: float32 [8192, 4096], P('arc', 'com')
- potentials_out: float32 [4096, 4096], P('arc', 'com')
The draws below stay inside these ranges and needn't reach their ends.
Inputs may be any that keep to these rules, and one draw needn't show every extreme that they name: `nodes_of`: arc block a names only node blocks (p - 1) * 4 to (p + 2) * 4 - 1, taken modulo 32, where p = a // 8.
All inputs are finite; a program needn't handle non-finite values.
Results may differ from the reference program's by a relative error of at most 0.0003.
Values sent between devices are 32-bit elements; how exact they have to be, the bound alone decides.
No kernel may reach another device: no remote copies, remote signals or barrier semaphores. Data moves between devices by JAX's collectives and lax.ppermute only.
A program may use at most 128 MiB of HBM per device.

```python
import math
import jax
import jax.numpy as jnp
from jax import lax

K = 4096
BLK = 128
AB_DEV = 8
NB_DEV = 4
DEG = 8
NPAT = 16
NW = 8
ITERS = 2
ABLK = 64
NBLK = 32


def draw_nodes_of(key, part):
    offsets = jax.random.randint(key, (ABLK, DEG), 0, 3 * NB_DEV).astype(jnp.int32)
    offsets = offsets.at[0, 0].set(NB_DEV - 1)
    offsets = offsets.at[0, 1].set(NB_DEV)
    owner = (jnp.arange(ABLK, dtype=jnp.int32) // AB_DEV)[:, None]
    return jnp.mod((owner - 1) * NB_DEV + offsets, NBLK).astype(jnp.int32)


def touch_ends(result, stream_key, smallest, top_value):
    dims = result.shape
    spot = [jax.random.randint(jax.random.fold_in(stream_key, axis), (), 0, dims[axis]) for axis in range(len(dims))]
    result = result.at[tuple(spot)].set(smallest)
    longest = dims.index(max(dims))
    spot[longest] = (spot[longest] + 1) % dims[longest]
    return result.at[tuple(spot)].set(top_value)


def levels(rng, dims, split, low, top_value):
    def one(axis_at, shards_of):
        draws = jax.random.uniform(jax.random.fold_in(jax.random.fold_in(rng, 6), axis_at), (shards_of,), jnp.float32, low / len(split), top_value / len(split))
        return jnp.repeat(jnp.exp(draws), dims[axis_at] // shards_of).reshape((-1,) + (1,) * (len(dims) - axis_at - 1))

    loudness = one(*split[0])
    for cut in split[1:]:
        loudness = loudness * one(*cut)
    return loudness


def scatter_about(rng, dims, spread, most, cuts=(), kind=jnp.bfloat16):
    entries = spread * jax.random.normal(rng, dims, jnp.float32)
    if cuts:
        entries = entries * levels(rng, dims, cuts, -0.22, 0.18)
    return jnp.clip(entries, -most, most).astype(kind)


def setup_inputs(seed: int = 0) -> dict:
    splits = jax.random.split(jax.random.key(seed), 12)
    flows = scatter_about(splits[0], (ABLK * BLK, K), 1.0, 6.0, ((0, 8), (1, 4)), jnp.float32)
    duals = scatter_about(splits[1], (ABLK * BLK, K), 1.0, 6.0, ((0, 8), (1, 4)), jnp.float32)
    potentials = scatter_about(splits[2], (NBLK * BLK, K), 1.0, 6.0, ((0, 8), (1, 4)), jnp.float32)
    demand = scatter_about(splits[3], (NBLK * BLK, K), 1.0, 6.0, ((0, 8), (1, 4)), jnp.float32)
    arc_cost = jnp.clip(0.2 + 0.8 * jax.random.uniform(splits[4], (ABLK * BLK,), jnp.float32) ** levels(splits[4], (ABLK * BLK,), ((0, 8),), -0.2, 0.2), 0.2, 1.0)
    cap_ratio = jnp.clip(jnp.exp(math.log(2.6) - 1.466337 * jax.random.uniform(splits[5], (ABLK * BLK,), jnp.float32) ** levels(splits[5], (ABLK * BLK,), ((0, 8),), -0.2, 0.2)), 0.6, 2.6)
    patterns = scatter_about(splits[6], (NPAT, BLK, BLK), (BLK * DEG) ** -0.5, 0.1875, (), jnp.float32)
    nodes_of = draw_nodes_of(jax.random.fold_in(splits[11], 71), 0)
    pattern_of = touch_ends(jax.random.randint(splits[8], (ABLK, DEG), 0, NPAT), jax.random.fold_in(splits[8], 1), 0, NPAT - 1).astype(jnp.int32)
    scen_index = touch_ends(jax.random.randint(splits[9], (K,), 0, NW), jax.random.fold_in(splits[9], 1), 0, NW - 1).astype(jnp.int32)
    level_weights = jnp.clip(jnp.exp(jax.random.uniform(splits[10], (NW,), jnp.float32, math.log(0.5), math.log(2.0))), 0.5, 2.0)
    return {"flows": flows, "duals": duals, "potentials": potentials, "demand": demand, "arc_cost": arc_cost, "cap_ratio": cap_ratio, "patterns": patterns, "nodes_of": nodes_of, "pattern_of": pattern_of, "scen_index": scen_index, "level_weights": level_weights}


penalty = 1.5
step_dual = 0.25
epsilon = 1e-06

def pull_arcs(potentials, patterns, nodes_of, pattern_of):
    node_tiles = potentials.reshape(NBLK, BLK, K)

    def one_block(item):
        nodes, kinds = item
        return jnp.einsum('dij,dik->jk', patterns[kinds], node_tiles[nodes], precision=lax.Precision.HIGHEST)
    pulled = lax.map(one_block, (nodes_of, pattern_of))
    return pulled.reshape(ABLK * BLK, K)

def push_nodes(flows, patterns, nodes_of, pattern_of):
    arc_tiles = flows.reshape(ABLK, BLK, K)

    def one_step(total, item):
        nodes, kinds, tile = item
        contrib = jnp.einsum('dij,jk->dik', patterns[kinds], tile, precision=lax.Precision.HIGHEST)
        return (total.at[nodes].add(contrib), None)
    start = jnp.zeros((NBLK, BLK, K), jnp.float32)
    total, _ = lax.scan(one_step, start, (nodes_of, pattern_of, arc_tiles))
    return total.reshape(NBLK * BLK, K)

def reference(flows, duals, potentials, demand, arc_cost, cap_ratio, patterns, nodes_of, pattern_of, scen_index, level_weights):
    weights = level_weights[scen_index]
    radius = cap_ratio * math.sqrt(K)
    for step in range(ITERS):
        pulled = pull_arcs(potentials, patterns, nodes_of, pattern_of)
        proposal = jnp.maximum(flows - duals - (arc_cost[:, None] * weights[None, :] + pulled) / penalty, 0.0)
        merged = proposal + duals
        squares = lax.optimization_barrier(jnp.sum(jnp.square(merged * weights[None, :]), axis=1))
        factor = jnp.minimum(1.0, radius / jnp.sqrt(squares + epsilon))
        flows = merged * factor[:, None]
        duals = merged - flows
        pushed = push_nodes(flows, patterns, nodes_of, pattern_of)
        potentials = potentials + step_dual * (pushed - demand)
    return (flows, duals, potentials)
```

```python
import functools
import math

import jax
import jax.numpy as jnp
from jax import lax
from jax.experimental import pallas as pl
from jax.experimental.pallas import tpu as pltpu
from jax.sharding import PartitionSpec as P

ITERS = 2
CHUNKS = 4

penalty = 1.5
step_dual = 0.25
epsilon = 1e-06

F32 = jnp.float32
BF16 = jnp.bfloat16
MIB = 1 << 20


def split(x):
    high = x.astype(BF16)
    return high, (x - high.astype(F32)).astype(BF16)


def product(a_high, a_low, x):
    x_high, x_low = split(x)
    dot = functools.partial(jnp.dot, preferred_element_type=F32)
    return dot(a_high, x_high) + (dot(a_low, x_high) + dot(a_high, x_low))


def call(kernel, out_shape, *, grid, in_specs, out_specs, flops, scratch=(), prefetch=0, limit=40):
    flat = jax.tree.leaves(out_shape)
    moved = sum(math.prod(s.shape) * s.dtype.itemsize for s in flat)
    return pl.pallas_call(
        kernel,
        out_shape=out_shape,
        grid_spec=pltpu.PrefetchScalarGridSpec(
            num_scalar_prefetch=prefetch,
            grid=grid,
            in_specs=in_specs,
            out_specs=out_specs,
            scratch_shapes=list(scratch),
        ),
        compiler_params=pltpu.CompilerParams(vmem_limit_bytes=limit * MIB),
        cost_estimate=pl.CostEstimate(flops=flops, bytes_accessed=2 * moved, transcendentals=0),
    )


def shape(*dims, dtype=F32):
    return jax.ShapeDtypeStruct(dims, dtype)


def block(dims, *index):
    return pl.BlockSpec(dims, lambda *_: index)


def build_kernel(slots, kinds, patterns, cost, gain_high, gain_low, turn_high, turn_low, cost_col, flipped, tall, wide):
    a = pl.program_id(0)
    count, size = patterns.shape[0], patterns.shape[1]
    listed = slots.shape[1]
    slabs = tall.shape[0]

    @pl.when(a == 0)
    def _():
        for k in range(count):
            flipped[k] = patterns[k].T

    tall[...] = jnp.zeros_like(tall)
    wide[...] = jnp.zeros_like(wide)
    for j in range(listed):
        slot, kind = slots[a, j], kinds[a, j]
        tall[slot] += patterns[kind]
        wide[slot] += flipped[kind]
    for s in range(slabs):
        rows = pl.ds(s * size, size)
        gain_high[rows, :], gain_low[rows, :] = split(tall[s])
        turn_high[:, rows], turn_low[:, rows] = split(wide[s])
    cost_col[...] = jnp.broadcast_to(cost[pl.ds(a, 1), :], (size, size)).T


def build(patterns, slots, kinds, cost):
    count, size, _ = patterns.shape
    arc_blocks = slots.shape[0]
    arcs = arc_blocks * size

    def run(slabs):
        nodes = slabs * size
        return call(
            build_kernel,
            (
                shape(nodes, arcs, dtype=BF16),
                shape(nodes, arcs, dtype=BF16),
                shape(arcs, nodes, dtype=BF16),
                shape(arcs, nodes, dtype=BF16),
                shape(arcs, size),
            ),
            grid=(arc_blocks,),
            in_specs=[
                pl.BlockSpec((count, size, size), lambda a, *_: (0, 0, 0)),
                pl.BlockSpec((arc_blocks, size), lambda a, *_: (0, 0)),
            ],
            out_specs=(
                pl.BlockSpec((nodes, size), lambda a, *_: (0, a)),
                pl.BlockSpec((nodes, size), lambda a, *_: (0, a)),
                pl.BlockSpec((size, nodes), lambda a, *_: (a, 0)),
                pl.BlockSpec((size, nodes), lambda a, *_: (a, 0)),
                pl.BlockSpec((size, size), lambda a, *_: (a, 0)),
            ),
            scratch=(
                pltpu.VMEM((count, size, size), F32),
                pltpu.VMEM((slabs, size, size), F32),
                pltpu.VMEM((slabs, size, size), F32),
            ),
            prefetch=2,
            flops=0,
        )(slots, kinds, patterns, cost)

    return run


def pull_own_kernel(turn_high, turn_low, x, out):
    out[...] = product(turn_high[...], turn_low[...], x[...])


def pull_add_kernel(turn_high, turn_low, x, base, out):
    out[...] = base[...] + product(turn_high[...], turn_low[...], x[...])


def pull_pair_kernel(turn_high, turn_low, kept, arrived, other, out, own):
    n = kept.shape[0]
    mine = kept[...] + step_dual * arrived[...]
    own[...] = mine
    out[...] = product(turn_high[:, :n], turn_low[:, :n], mine) + product(
        turn_high[:, n:], turn_low[:, n:], other[...]
    )


def finish(pulled, parts, cost, weight, sums, merged_ref, sums_ref):
    lanes = cost.shape[1]
    total = None
    for h in range(pulled.shape[1] // lanes):
        cols = slice(h * lanes, (h + 1) * lanes)
        flow, dual = parts(cols)
        w = weight[:, cols]
        price = (cost * w + pulled[:, cols]) * (1.0 / penalty)
        merged = jnp.maximum(flow - dual - price, 0.0) + dual
        merged_ref[:, cols] = merged
        scaled = merged * w
        squares = scaled * scaled
        total = squares if total is None else total + squares
    rows = lax.dot_general(
        jnp.ones((8, lanes), F32),
        total,
        (((1,), (1,)), ((), ())),
        precision=lax.Precision.HIGHEST,
        preferred_element_type=F32,
    )
    sums_ref[...] = sums + rows[:1]


def pull_first_kernel(turn_high, turn_low, x, base, cost, weight, sums, flows, duals, merged_ref, sums_ref):
    pulled = base[...] + product(turn_high[...], turn_low[...], x[...])
    finish(pulled, lambda c: (flows[:, c], duals[:, c]), cost[...], weight[...], sums[...], merged_ref, sums_ref)


def pull_later_kernel(turn_high, turn_low, x, base, cost, weight, sums, before, factor, merged_ref, sums_ref):
    pulled = base[...] + product(turn_high[...], turn_low[...], x[...])

    def parts(c):
        flow = before[:, c] * factor[...]
        return flow, before[:, c] - flow

    finish(pulled, parts, cost[...], weight[...], sums[...], merged_ref, sums_ref)


def column_factor(total, radius):
    row = jnp.minimum(1.0, radius / jnp.sqrt(total + epsilon))
    lanes = 128
    pieces = [
        jnp.broadcast_to(row[:, i : i + lanes], (lanes, lanes)).T for i in range(0, row.shape[1], lanes)
    ]
    return jnp.concatenate(pieces, axis=0)


def push_body(gain_high, gain_low, merged, factor, kept, demand, far, near, own):
    lanes = factor.shape[1]
    flow = jnp.concatenate(
        [merged[:, h : h + lanes] * factor for h in range(0, merged.shape[1], lanes)], axis=1
    )
    n = far.shape[0]
    out = product(gain_high[...], gain_low[...], flow)
    own[...] = kept[...] + step_dual * (out[:n] - demand[...])
    near[...] = out[n : 2 * n]
    far[...] = out[2 * n :]


def push_first_kernel(gain_high, gain_low, merged, total, radius, kept, demand, far, near, own, factor):
    f = column_factor(total[...], radius[...])
    factor[...] = f
    push_body(gain_high, gain_low, merged[...], f, kept, demand, far, near, own)


def push_next_kernel(gain_high, gain_low, merged, factor, kept, demand, far, near, own):
    push_body(gain_high, gain_low, merged[...], factor[...], kept, demand, far, near, own)


def output_kernel(factor, *refs):
    merged, (flows, duals) = refs[:-2], refs[-2:]
    width = merged[0].shape[1]
    lanes = factor.shape[1]
    for c, m in enumerate(merged):
        for h in range(0, width, lanes):
            cols = slice(c * width + h, c * width + h + lanes)
            value = m[:, h : h + lanes]
            flow = value * factor[...]
            flows[:, cols] = flow
            duals[:, cols] = value - flow


def total_over(x, axis):
    size = lax.axis_size(axis)
    if size & (size - 1):
        return lax.psum(x, axis)
    step = 1
    while step < size:
        x = x + lax.ppermute(x, axis, [(i, i ^ step) for i in range(size)])
        step *= 2
    return x


def per_device(
    flows,
    duals,
    potentials,
    demand,
    arc_cost,
    cap_ratio,
    patterns,
    nodes_of,
    pattern_of,
    scen_index,
    level_weights,
):
    size = patterns.shape[1]
    arcs, columns = flows.shape
    nodes = potentials.shape[0]
    arc_blocks = nodes_of.shape[0]
    node_blocks = nodes // size
    ring = lax.axis_size("arc")
    position = lax.axis_index("arc")
    width = columns // CHUNKS
    chunks = range(CHUNKS)

    swap = [(i, i ^ 1) for i in range(ring)]
    onward = [(i, (i + 2) % ring if i % 2 == 0 else (i - 2) % ring) for i in range(ring)]
    backward = [(b, a) for a, b in onward]

    distance = jnp.mod(nodes_of // node_blocks - position, ring)
    near = jnp.where(position % 2 == 0, 1, ring - 1)
    group = jnp.where(distance == 0, 0, jnp.where(distance == near, 1, 2))
    slots = group * node_blocks + nodes_of % node_blocks

    gain_high, gain_low, turn_high, turn_low, cost = build(
        patterns, slots, pattern_of, arc_cost.reshape(arc_blocks, size)
    )(3 * node_blocks)

    mine = lax.dynamic_slice_in_dim(scen_index, lax.axis_index("com") * columns, columns)
    levels = jnp.arange(level_weights.shape[0], dtype=jnp.int32)
    weight = jnp.sum(
        jnp.where(mine[None, :] == levels[:, None], level_weights[:, None], 0.0), axis=0
    ).reshape(1, columns)
    radius = (cap_ratio * math.sqrt(columns * lax.axis_size("com"))).reshape(1, arcs)

    turn_spec = lambda g, k=1: block((arcs, k * nodes), 0, g)
    work = 6 * arcs * nodes * width

    def send(x, route):
        return lax.ppermute(x, "arc", route)

    close = [send(lax.slice_in_dim(potentials, c * width, (c + 1) * width, axis=1), swap) for c in chunks]
    far = [send(close[c], onward) for c in chunks]

    own_pull = call(
        pull_own_kernel,
        shape(arcs, columns),
        grid=(CHUNKS,),
        in_specs=[turn_spec(0), turn_spec(0), pl.BlockSpec((nodes, width), lambda c: (0, c))],
        out_specs=pl.BlockSpec((arcs, width), lambda c: (0, c)),
        flops=work * CHUNKS,
    )(turn_high, turn_low, potentials)
    pulled = [
        call(
            pull_add_kernel,
            shape(arcs, width),
            grid=(1,),
            in_specs=[turn_spec(1), turn_spec(1), block((nodes, width), 0, 0), block((arcs, width), 0, c)],
            out_specs=block((arcs, width), 0, 0),
            flops=work,
        )(turn_high, turn_low, close[c], own_pull)
        for c in chunks
    ]
    kept = [potentials] * CHUNKS
    before = None
    factor = None
    for step in range(ITERS):
        sums = jnp.zeros((1, arcs), F32)
        merged = []
        for c in chunks:
            first = step == 0
            state = (flows, duals) if first else (before[c], factor)
            state_specs = (
                [block((arcs, width), 0, c)] * 2
                if first
                else [block((arcs, width), 0, 0), block((arcs, size), 0, 0)]
            )
            m, sums = call(
                pull_first_kernel if first else pull_later_kernel,
                (shape(arcs, width), shape(1, arcs)),
                grid=(1,),
                in_specs=[
                    turn_spec(2),
                    turn_spec(2),
                    block((nodes, width), 0, 0),
                    block((arcs, width), 0, 0),
                    block((arcs, size), 0, 0),
                    block((1, width), 0, c),
                    block((1, arcs), 0, 0),
                    *state_specs,
                ],
                out_specs=(block((arcs, width), 0, 0), block((1, arcs), 0, 0)),
                flops=work,
            )(turn_high, turn_low, far[c], pulled[c], cost, weight, sums, *state)
            merged.append(m)
        total = total_over(sums, "com")

        spilled, shared, held = [], [], []
        for c in chunks:
            first = c == 0
            extra = (total, radius) if first else (factor,)
            extra_specs = [block((1, arcs), 0, 0)] * 2 if first else [block((arcs, size), 0, 0)]
            outs = call(
                push_first_kernel if first else push_next_kernel,
                (shape(nodes, width),) * 3 + ((shape(arcs, size),) if first else ()),
                grid=(1,),
                in_specs=[
                    block((3 * nodes, arcs), 0, 0),
                    block((3 * nodes, arcs), 0, 0),
                    block((arcs, width), 0, 0),
                    *extra_specs,
                    block((nodes, width), 0, c if step == 0 else 0),
                    block((nodes, width), 0, c),
                ],
                out_specs=(block((nodes, width), 0, 0),) * 3
                + ((block((arcs, size), 0, 0),) if first else ()),
                flops=3 * work,
            )(gain_high, gain_low, merged[c], *extra, kept[c], demand)
            if first:
                factor = outs[3]
            spilled.append(outs[0])
            shared.append(outs[1])
            held.append(outs[2])
        before = merged

        passed = [send(spilled[c], backward) for c in chunks]
        if step == ITERS - 1:
            arrived = [send(shared[c] + passed[c], swap) for c in chunks]
            potentials = jnp.concatenate([held[c] + step_dual * arrived[c] for c in chunks], axis=1)
            break
        theirs = [send(held[c], swap) for c in chunks]
        ours = [shared[c] + passed[c] for c in chunks]
        close = [theirs[c] + step_dual * ours[c] for c in chunks]
        far = [send(close[c], onward) for c in chunks]
        arrived = [send(ours[c], swap) for c in chunks]
        pulled, kept = [], []
        for c in chunks:
            p, k = call(
                pull_pair_kernel,
                (shape(arcs, width), shape(nodes, width)),
                grid=(1,),
                in_specs=[turn_spec(0, 2), turn_spec(0, 2)] + [block((nodes, width), 0, 0)] * 3,
                out_specs=(block((arcs, width), 0, 0), block((nodes, width), 0, 0)),
                flops=2 * work,
            )(turn_high, turn_low, held[c], arrived[c], close[c])
            pulled.append(p)
            kept.append(k)

    tile = 128
    flows, duals = call(
        output_kernel,
        (shape(arcs, columns),) * 2,
        grid=(arcs // tile,),
        in_specs=[pl.BlockSpec((tile, size), lambda i: (i, 0))]
        + [pl.BlockSpec((tile, width), lambda i: (i, 0))] * CHUNKS,
        out_specs=(pl.BlockSpec((tile, columns), lambda i: (i, 0)),) * 2,
        flops=0,
    )(factor, *before)
    return (flows, duals, potentials)


def solution(mesh):
    placed = (
        P("arc", "com"),
        P("arc", "com"),
        P("arc", "com"),
        P("arc", "com"),
        P("arc"),
        P("arc"),
        P(),
        P("arc", None),
        P("arc", None),
        P(),
        P(),
    )
    return jax.shard_map(
        per_device,
        mesh=mesh,
        in_specs=placed,
        out_specs=(P("arc", "com"), P("arc", "com"), P("arc", "com")),
        check_vma=False,
    )
```

```python
import functools
import math

import jax
import jax.numpy as jnp
from jax import lax
from jax.experimental import pallas as pl
from jax.experimental.pallas import tpu as pltpu
from jax.sharding import PartitionSpec as P


ITERS = 2
CHUNKS = 4
GROUPS = 3

penalty = 1.5
step_dual = 0.25
epsilon = 1e-06

F32 = jnp.float32
BF16 = jnp.bfloat16
MIB = 1 << 20


def split(x):
    high = x.astype(BF16)
    return high, (x - high.astype(F32)).astype(BF16)


def product(a_high, a_low, x):
    x_high, x_low = split(x)
    dot = functools.partial(jnp.dot, preferred_element_type=F32)
    return dot(a_high, x_high) + (dot(a_low, x_high) + dot(a_high, x_low))


def call(kernel, out_shape, *, grid, in_specs, out_specs, flops, scratch=(), prefetch=0, limit=16):
    flat = jax.tree.leaves(out_shape)
    moved = sum(math.prod(s.shape) * s.dtype.itemsize for s in flat)
    run = pl.pallas_call(
        kernel,
        out_shape=out_shape,
        grid_spec=pltpu.PrefetchScalarGridSpec(
            num_scalar_prefetch=prefetch,
            grid=grid,
            in_specs=in_specs,
            out_specs=out_specs,
            scratch_shapes=list(scratch),
        ),
        compiler_params=pltpu.CompilerParams(vmem_limit_bytes=limit * MIB),
        cost_estimate=pl.CostEstimate(flops=flops, bytes_accessed=2 * moved, transcendentals=0),
    )
    return run


def shape(*dims, dtype=F32):
    return jax.ShapeDtypeStruct(dims, dtype)


def block(dims, *index):
    return pl.BlockSpec(dims, lambda *_: index)


def build_kernel(nodes_of, kinds, levels, patterns, cost, scen, gain_high, gain_low, *refs):
    turns, (cost_col, weight, flipped, tall, wide) = refs[:-5], refs[-5:]
    a = pl.program_id(0)
    count, size = patterns.shape[0], patterns.shape[1]
    listed = nodes_of.shape[1]
    slabs = tall.shape[0]
    mine = slabs // GROUPS
    ring, position = lax.axis_size("arc"), lax.axis_index("arc")
    side = jnp.where(lax.rem(position, 2) == 0, 1, ring - 1)

    @pl.when(a == 0)
    def _():
        for k in range(count):
            flipped[k] = patterns[k].T
        columns = weight.shape[1]
        first = pl.multiple_of(lax.axis_index("com") * columns, size)
        index = scen[:, pl.ds(first, columns)]
        total = jnp.zeros(index.shape, F32)
        for level in range(levels.shape[0]):
            total += jnp.where(index == level, levels[level], 0.0)
        weight[...] = total

    tall[...] = jnp.zeros_like(tall)
    wide[...] = jnp.zeros_like(wide)
    for j in range(listed):
        node, kind = nodes_of[a, j], kinds[a, j]
        distance = lax.rem(lax.div(node, mine) - position + ring, ring)
        group = jnp.where(distance == 0, 0, jnp.where(distance == side, 1, 2))
        slot = group * mine + lax.rem(node, mine)
        tall[slot] += patterns[kind]
        wide[slot] += flipped[kind]
    for s in range(slabs):
        rows = pl.ds(s * size, size)
        gain_high[rows, :], gain_low[rows, :] = split(tall[s])
        group, place = divmod(s, mine)
        cols = pl.ds(place * size, size)
        turns[2 * group][:, cols], turns[2 * group + 1][:, cols] = split(wide[s])
    cost_col[...] = jnp.broadcast_to(cost[pl.ds(a, 1), :], (size, size)).T


def build(patterns, nodes_of, kinds, levels, cost, scen, nodes, columns):
    count, size, _ = patterns.shape
    arc_blocks = nodes_of.shape[0]
    arcs = arc_blocks * size
    whole = lambda *dims: pl.BlockSpec(dims, lambda *_: (0,) * len(dims))
    part = lambda *dims: pl.BlockSpec(dims, lambda a, *_: (a, 0))
    return call(
        build_kernel,
        (
            *[shape(GROUPS * nodes, arcs, dtype=BF16)] * 2,
            *[shape(arcs, nodes, dtype=BF16)] * (2 * GROUPS),
            shape(arcs, size),
            shape(1, columns),
        ),
        grid=(arc_blocks,),
        in_specs=[whole(*patterns.shape), whole(*cost.shape), whole(*scen.shape)],
        out_specs=(
            *[pl.BlockSpec((GROUPS * nodes, size), lambda a, *_: (0, a))] * 2,
            *[part(size, nodes)] * (2 * GROUPS),
            part(size, size),
            whole(1, columns),
        ),
        scratch=(
            pltpu.VMEM((count, size, size), F32),
            *[pltpu.VMEM((GROUPS * nodes // size, size, size), F32)] * 2,
        ),
        prefetch=3,
        flops=0,
    )(nodes_of, kinds, levels, patterns, cost, scen)


def copy_kernel(x, out):
    out[...] = x[...]


def pull_own_kernel(turn_high, turn_low, x, out):
    out[...] = product(turn_high[...], turn_low[...], x[...])


def pull_pair_kernel(own_high, own_low, near_high, near_low, own, near, out):
    out[...] = product(own_high[...], own_low[...], own[...]) + product(
        near_high[...], near_low[...], near[...]
    )


def pull_total_kernel(turn_high, turn_low, kept, arrived, base, out, own):
    mine = kept[...] + step_dual * arrived[...]
    own[...] = mine
    out[...] = base[...] + product(turn_high[...], turn_low[...], mine)


def finish(pulled, parts, cost, weight, sums, merged_ref, sums_ref):
    lanes = cost.shape[1]
    total = None
    for h in range(pulled.shape[1] // lanes):
        cols = slice(h * lanes, (h + 1) * lanes)
        flow, dual = parts(cols)
        w = weight[:, cols]
        price = (cost * w + pulled[:, cols]) * (1.0 / penalty)
        merged = jnp.maximum(flow - dual - price, 0.0) + dual
        merged_ref[:, cols] = merged
        scaled = merged * w
        squares = scaled * scaled
        total = squares if total is None else total + squares
    rows = lax.dot_general(
        jnp.ones((8, lanes), F32),
        total,
        (((1,), (1,)), ((), ())),
        precision=lax.Precision.HIGHEST,
        preferred_element_type=F32,
    )
    sums_ref[...] = sums + rows[:1]


def pull_first_kernel(turn_high, turn_low, x, base, cost, weight, sums, flows, duals, merged_ref, sums_ref):
    pulled = base[...] + product(turn_high[...], turn_low[...], x[...])
    finish(pulled, lambda c: (flows[:, c], duals[:, c]), cost[...], weight[...], sums[...], merged_ref, sums_ref)


def pull_later_kernel(turn_high, turn_low, x, base, cost, weight, sums, before, factor, merged_ref, sums_ref):
    pulled = base[...] + product(turn_high[...], turn_low[...], x[...])

    def parts(c):
        flow = before[:, c] * factor[...]
        return flow, before[:, c] - flow

    finish(pulled, parts, cost[...], weight[...], sums[...], merged_ref, sums_ref)


def column_factor(total, radius):
    row = jnp.minimum(1.0, radius / jnp.sqrt(total + epsilon))
    lanes = 128
    pieces = [
        jnp.broadcast_to(row[:, i : i + lanes], (lanes, lanes)).T for i in range(0, row.shape[1], lanes)
    ]
    return jnp.concatenate(pieces, axis=0)


def push_body(gain_high, gain_low, merged, factor, kept, demand, far, near, own):
    lanes = factor.shape[1]
    flow = jnp.concatenate(
        [merged[:, h : h + lanes] * factor for h in range(0, merged.shape[1], lanes)], axis=1
    )
    n = far.shape[0]
    out = product(gain_high[...], gain_low[...], flow)
    own[...] = kept[...] + step_dual * (out[:n] - demand[...])
    near[...] = out[n : 2 * n]
    far[...] = out[2 * n :]


def push_first_kernel(scale, gain_high, gain_low, merged, total, ratio, kept, demand, far, near, own, factor):
    f = column_factor(total[...], ratio[...] * scale)
    factor[...] = f
    push_body(gain_high, gain_low, merged[...], f, kept, demand, far, near, own)


def push_next_kernel(gain_high, gain_low, merged, factor, kept, demand, far, near, own):
    push_body(gain_high, gain_low, merged[...], factor[...], kept, demand, far, near, own)


def output_kernel(factor, *refs):
    merged, (flows, duals) = refs[:-2], refs[-2:]
    width = merged[0].shape[1]
    lanes = factor.shape[1]
    for c, m in enumerate(merged):
        for h in range(0, width, lanes):
            cols = slice(c * width + h, c * width + h + lanes)
            value = m[:, h : h + lanes]
            flow = value * factor[...]
            flows[:, cols] = flow
            duals[:, cols] = value - flow


def total_over(x, axis):
    size = lax.axis_size(axis)
    if size & (size - 1):
        return lax.psum(x, axis)
    step = 1
    while step < size:
        x = x + lax.ppermute(x, axis, [(i, i ^ step) for i in range(size)])
        step *= 2
    return x


def per_device(
    flows,
    duals,
    potentials,
    demand,
    arc_cost,
    cap_ratio,
    patterns,
    nodes_of,
    pattern_of,
    scen_index,
    level_weights,
):
    size = patterns.shape[1]
    arcs, columns = flows.shape
    nodes = potentials.shape[0]
    arc_blocks = nodes_of.shape[0]
    ring = lax.axis_size("arc")
    width = columns // CHUNKS
    chunks = range(CHUNKS)

    swap = [(i, i ^ 1) for i in range(ring)]
    onward = [(i, (i + 2) % ring if i % 2 == 0 else (i - 2) % ring) for i in range(ring)]
    backward = [(b, a) for a, b in onward]

    gain_high, gain_low, *turns, cost, weight = build(
        patterns,
        nodes_of,
        pattern_of,
        level_weights,
        arc_cost.reshape(arc_blocks, size),
        scen_index.reshape(1, -1),
        nodes,
        columns,
    )
    turn_own, turn_near, turn_far = turns[:2], turns[2:4], turns[4:]
    ratio = cap_ratio.reshape(1, arcs)
    scale = math.sqrt(columns * lax.axis_size("com"))

    turn_specs = [block((arcs, nodes), 0, 0)] * 2
    work = 6 * arcs * nodes * width

    def send(x, route):
        return lax.ppermute(x, "arc", route)

    pieces = [
        call(
            copy_kernel,
            shape(nodes, width),
            grid=(1,),
            in_specs=[block((nodes, width), 0, c)],
            out_specs=block((nodes, width), 0, 0),
            flops=0,
        )(potentials)
        for c in chunks
    ]
    close = [send(pieces[c], swap) for c in chunks]
    far = [send(close[c], onward) for c in chunks]
    pulled = [
        call(
            pull_pair_kernel,
            shape(arcs, width),
            grid=(1,),
            in_specs=turn_specs * 2 + [block((nodes, width), 0, 0)] * 2,
            out_specs=block((arcs, width), 0, 0),
            flops=2 * work,
        )(*turn_own, *turn_near, pieces[c], close[c])
        for c in chunks
    ]
    kept = pieces
    before = None
    factor = None
    for step in range(ITERS):
        sums = jnp.zeros((1, arcs), F32)
        merged = []
        for c in chunks:
            first = step == 0
            state = (flows, duals) if first else (before[c], factor)
            state_specs = (
                [block((arcs, width), 0, c)] * 2
                if first
                else [block((arcs, width), 0, 0), block((arcs, size), 0, 0)]
            )
            m, sums = call(
                pull_first_kernel if first else pull_later_kernel,
                (shape(arcs, width), shape(1, arcs)),
                grid=(1,),
                in_specs=[
                    *turn_specs,
                    block((nodes, width), 0, 0),
                    block((arcs, width), 0, 0),
                    block((arcs, size), 0, 0),
                    block((1, width), 0, c),
                    block((1, arcs), 0, 0),
                    *state_specs,
                ],
                out_specs=(block((arcs, width), 0, 0), block((1, arcs), 0, 0)),
                flops=work,
            )(*turn_far, far[c], pulled[c], cost, weight, sums, *state)
            merged.append(m)
        total = total_over(sums, "com")

        spilled, shared, held = [], [], []
        for c in chunks:
            first = c == 0
            extra = (total, ratio) if first else (factor,)
            extra_specs = [block((1, arcs), 0, 0)] * 2 if first else [block((arcs, size), 0, 0)]
            outs = call(
                functools.partial(push_first_kernel, scale) if first else push_next_kernel,
                (shape(nodes, width),) * 3 + ((shape(arcs, size),) if first else ()),
                grid=(1,),
                in_specs=[
                    block((3 * nodes, arcs), 0, 0),
                    block((3 * nodes, arcs), 0, 0),
                    block((arcs, width), 0, 0),
                    *extra_specs,
                    block((nodes, width), 0, 0),
                    block((nodes, width), 0, c),
                ],
                out_specs=(block((nodes, width), 0, 0),) * 3
                + ((block((arcs, size), 0, 0),) if first else ()),
                flops=3 * work,
            )(gain_high, gain_low, merged[c], *extra, kept[c], demand)
            if first:
                factor = outs[3]
            spilled.append(outs[0])
            shared.append(outs[1])
            held.append(outs[2])
        before = merged

        passed = [send(spilled[c], backward) for c in chunks]
        if step == ITERS - 1:
            arrived = [send(shared[c] + passed[c], swap) for c in chunks]
            potentials = jnp.concatenate([held[c] + step_dual * arrived[c] for c in chunks], axis=1)
            break
        theirs = [send(held[c], swap) for c in chunks]
        ours = [shared[c] + passed[c] for c in chunks]
        close = [theirs[c] + step_dual * ours[c] for c in chunks]
        far = [send(close[c], onward) for c in chunks]
        arrived = [send(ours[c], swap) for c in chunks]
        pulled, kept = [], []
        for c in chunks:
            p = call(
                pull_own_kernel,
                shape(arcs, width),
                grid=(1,),
                in_specs=turn_specs + [block((nodes, width), 0, 0)],
                out_specs=block((arcs, width), 0, 0),
                flops=work,
            )(*turn_near, close[c])
            p, k = call(
                pull_total_kernel,
                (shape(arcs, width), shape(nodes, width)),
                grid=(1,),
                in_specs=turn_specs
                + [block((nodes, width), 0, 0)] * 2
                + [block((arcs, width), 0, 0)],
                out_specs=(block((arcs, width), 0, 0), block((nodes, width), 0, 0)),
                flops=work,
            )(*turn_own, held[c], arrived[c], p)
            pulled.append(p)
            kept.append(k)

    tile = 128
    flows, duals = call(
        output_kernel,
        (shape(arcs, columns),) * 2,
        grid=(arcs // tile,),
        in_specs=[pl.BlockSpec((tile, size), lambda i: (i, 0))]
        + [pl.BlockSpec((tile, width), lambda i: (i, 0))] * CHUNKS,
        out_specs=(pl.BlockSpec((tile, columns), lambda i: (i, 0)),) * 2,
        flops=0,
    )(factor, *before)
    return (flows, duals, potentials)


def solution(mesh):
    placed = (
        P("arc", "com"),
        P("arc", "com"),
        P("arc", "com"),
        P("arc", "com"),
        P("arc"),
        P("arc"),
        P(),
        P("arc", None),
        P("arc", None),
        P(),
        P(),
    )
    return jax.shard_map(
        per_device,
        mesh=mesh,
        in_specs=placed,
        out_specs=(P("arc", "com"), P("arc", "com"), P("arc", "com")),
        check_vma=False,
    )
```
